32 devices in a mesh: fn: 8 (over z, x), sub: 4 (over y, core).
Axes of the slice: x: 2, y: 2, z: 4, core: 2. Of those that a mesh axis runs over, the one named last changes fastest.
Arguments:
- coeffs: float32 [1024, 4, 16, 128], P('fn', None, 'sub'), may hold values from -6 to 6
- offsets: int32 [1024], replicated, may hold values from 0 to 127, as said below
- potential: float32 [128, 16, 128], P(None, 'sub'), may hold values from -1.5 to 1.5
Outputs:
- gradient: float32 [1024, 4, 16, 128], P('fn', None, 'sub')
The draws below stay inside these ranges and needn't reach their ends.
Inputs may be any that keep to these rules, and one draw needn't show every extreme that they name: `offsets`: Nondecreasing; each grid plane is the first plane of 1 to 15 boxes, both ends reached, on average 8; at most 46 boxes cover any plane (boxes wrap around the periodic wire), and some plane is covered by exactly 46.
All inputs are finite; a program needn't handle non-finite values.
Results may differ from the reference program's by a relative error of at most 0.0003.
Values sent between devices are 32-bit elements; how exact they have to be, the bound alone decides.
A program may use at most 64 MiB of HBM per device.

```python
import jax
import jax.numpy as jnp
from jax import lax

FN_DEV = 128
PB = 4
CY = 16
CZ = 128
DENS = 8
SWING = 7
NF = 1024
NB = 128
KMAX = 46
N_FN = 8


def draw_offsets(key, part):
    move_key, spot_key = jax.random.split(key)
    step_sizes = jax.random.randint(move_key, (NB,), -SWING, SWING + 1).astype(jnp.int32)
    center = jax.random.randint(spot_key, (), 6, NB - 1).astype(jnp.int32)
    planted = jnp.array([0, -SWING, -SWING, -SWING, 0, SWING, SWING], jnp.int32)
    plane_ids = jnp.arange(NB, dtype=jnp.int32)
    from_start = plane_ids - (center - 6)
    in_plant = (from_start >= 0) & (from_start < 7)
    plant_values = planted[jnp.clip(from_start, 0, 6)]
    closing = plane_ids == NB - 1

    def advance(earlier, inputs):
        step_size, forced, forced_value, is_closing = inputs
        level = jnp.clip(earlier + step_size, -SWING, SWING).astype(jnp.int32)
        level = jnp.where(forced, forced_value, level)
        level = jnp.where(is_closing, jnp.int32(0), level).astype(jnp.int32)
        return (level, level)
    _, levels = lax.scan(advance, jnp.int32(0), (step_sizes, in_plant, plant_values, closing))
    counts = (DENS + levels - jnp.roll(levels, 1)).astype(jnp.int32)
    endings = jnp.cumsum(counts).astype(jnp.int32)
    func_ids = jnp.arange(NF, dtype=jnp.int32)
    return jnp.searchsorted(endings, func_ids, side='right').astype(jnp.int32)


def block_scale(rng, extent, pieces, least, largest):
    def one(position, shards_of):
        steps = jax.random.uniform(jax.random.fold_in(jax.random.fold_in(rng, 6), position), (shards_of,), jnp.float32, least / len(pieces), largest / len(pieces))
        return jnp.repeat(jnp.exp(steps), extent[position] // shards_of).reshape((-1,) + (1,) * (len(extent) - position - 1))

    loudness = one(*pieces[0])
    for cut in pieces[1:]:
        loudness = loudness * one(*cut)
    return loudness


def noise(stream_key, shape, scale, reach, cuts=(), kind=jnp.bfloat16):
    gain = block_scale(stream_key, shape, cuts, -0.22, 0.18) if cuts else 1.0
    entries = jax.random.normal(stream_key, shape, jnp.float32) * scale * gain
    return jnp.minimum(jnp.maximum(entries, -reach), reach).astype(kind)


def setup_inputs(seed: int = 0) -> dict:
    splits = jax.random.split(jax.random.key(seed), 4)
    coeffs = noise(splits[0], (NF, PB, CY, CZ), 1.0, 6.0, ((0, 8), (2, 4)), jnp.float32)
    offsets = draw_offsets(jax.random.fold_in(splits[3], 71), 0)
    potential = jnp.clip(jax.random.uniform(splits[2], (NB, CY, CZ), jnp.float32, -1.5, 1.5) * block_scale(splits[2], (NB, CY, CZ), ((1, 4),), -0.4, 0.0), -1.5, 1.5)
    return {"coeffs": coeffs, "offsets": offsets, "potential": potential}


penalty = 0.5
highest = lax.Precision.HIGHEST


def kinetic(box_data, padded_y):
    padded_x = jnp.pad(box_data, ((0, 0), (1, 1), (0, 0), (0, 0)))
    padded_z = jnp.pad(box_data, ((0, 0), (0, 0), (0, 0), (1, 1)))
    beside = padded_x[:, 2:] + padded_x[:, :-2]
    beside = beside + padded_y[:, :, 2:] + padded_y[:, :, :-2]
    beside = beside + padded_z[..., 2:] + padded_z[..., :-2]
    return -0.5 * (beside - 6.0 * box_data)


def to_band(gram_block):
    width = gram_block.shape[0]
    row_ids = jnp.arange(width, dtype=jnp.int32)[:, None]
    col_ids = row_ids + jnp.arange(128, dtype=jnp.int32)[None, :] - 64
    inside = (col_ids >= 0) & (col_ids < width)
    picked = jnp.take_along_axis(gram_block, jnp.clip(col_ids, 0, width - 1), axis=1)
    return jnp.where(inside, picked, 0.0)


def from_band(band_rows):
    width = band_rows.shape[0]
    index_map = jnp.arange(width, dtype=jnp.int32)[None, :] - jnp.arange(width, dtype=jnp.int32)[:, None] + 64
    return jnp.take_along_axis(band_rows, index_map, axis=1)


def reference(coeffs, offsets, potential):
    total_funcs = coeffs.shape[0]
    func_ids = jnp.arange(total_funcs, dtype=jnp.int32)
    row_of = (func_ids % N_FN) * FN_DEV + func_ids // N_FN
    box_data = coeffs[row_of]
    padded_y = jnp.pad(box_data, ((0, 0), (0, 0), (1, 1), (0, 0)))
    box_planes = (offsets[:, None] + jnp.arange(PB, dtype=jnp.int32)[None, :]) % NB
    applied = kinetic(box_data, padded_y) + potential[box_planes] * box_data
    bounds = jnp.searchsorted(offsets, jnp.arange(NB + 1, dtype=jnp.int32), side="left").astype(jnp.int32)
    counts = bounds[1:] - bounds[:-1]
    firsts = bounds[:-1]
    plane_all = jnp.arange(NB, dtype=jnp.int32)
    first_rows = firsts[(plane_all - (PB - 1)) % NB]
    live_counts = jnp.zeros((NB,), jnp.int32)
    for back_step in range(PB):
        live_counts = live_counts + counts[(plane_all - back_step) % NB]
    slot_range = jnp.arange(KMAX, dtype=jnp.int32)
    volume = 1.0 / (PB * CY * CZ)

    def plane_data(plane_id):
        is_live = slot_range < live_counts[plane_id]
        members = (first_rows[plane_id] + slot_range) % total_funcs
        piece_index = (plane_id - offsets[members]) % NB
        values = box_data[members, piece_index].reshape(KMAX, CY * CZ) * is_live[:, None]
        images = applied[members, piece_index].reshape(KMAX, CY * CZ) * is_live[:, None]
        return members, piece_index, is_live, values, images

    def plane_band(plane_id):
        members, piece_index, is_live, values, images = plane_data(plane_id)
        gram_block = volume * jnp.dot(values, (images - penalty * values).T, precision=highest)
        return to_band(gram_block), jnp.where(is_live, members, total_funcs)

    blocks, targets = lax.map(plane_band, plane_all)
    band_rows = jnp.zeros((total_funcs, 128), jnp.float32).at[targets.reshape(-1)].add(blocks.reshape(-1, 128), mode="drop")

    def plane_step(plane_id, gradients):
        members, piece_index, is_live, values, images = plane_data(plane_id)
        mixing = from_band(band_rows[members]) * is_live[None, :]
        update = images - jnp.dot(mixing, values, precision=highest) - penalty * values
        target = jnp.where(is_live, members, total_funcs)
        return gradients.at[target, piece_index].set(update.reshape(KMAX, CY, CZ), mode="drop")

    gradients = lax.fori_loop(0, NB, plane_step, jnp.zeros_like(box_data))
    row_ids = jnp.arange(total_funcs, dtype=jnp.int32)
    func_of_row = (row_ids % FN_DEV) * N_FN + row_ids // FN_DEV
    return gradients[func_of_row]
```

```python
import jax
import jax.numpy as jnp
from jax import lax
from jax.sharding import PartitionSpec as P

KMAX = 46
penalty = 0.5
highest = lax.Precision.HIGHEST


def sub_edges(cells):
    count = lax.axis_size("sub")
    up = [(i, i + 1) for i in range(count - 1)]
    down = [(i + 1, i) for i in range(count - 1)]
    rows = cells.shape[2]
    above = lax.ppermute(cells[:, :, rows - 1 : rows], "sub", up)
    below = lax.ppermute(cells[:, :, 0:1], "sub", down)
    return above, below


def sub_sum(part):
    count = lax.axis_size("sub")
    step = 1
    while step < count:
        part = part + lax.ppermute(part, "sub", [(i, i ^ step) for i in range(count)])
        step *= 2
    return part


def body(coeffs, offsets, potential):
    n = lax.axis_size("fn")
    e = lax.axis_index("fn")
    local, box, rows, depth = coeffs.shape
    planes = potential.shape[0]
    cells = rows * depth
    m = local // n
    h = -(-(KMAX - 1) // n)
    win = m + 2 * h
    volume = 1.0 / (box * 16 * 128)
    ext = jnp.concatenate([coeffs[local - h :], coeffs, coeffs[:h]], axis=0)
    send = jnp.stack([ext[m * k : m * k + win] for k in range(n)], axis=0)
    got = lax.all_to_all(send.reshape(n, win, box, cells), "fn", 0, 0, tiled=True)

    offs = offsets.reshape(local, n)
    offs = jnp.concatenate([offs[local - h :], offs, offs[:h]], axis=0)
    woff = lax.dynamic_slice_in_dim(offs, m * e, win, axis=0).T
    ooff = woff[:, h : h + m].reshape(-1)
    woff = woff.reshape(-1)

    own = got[:, h : h + m].reshape(local, box, rows, depth)
    above, below = sub_edges(own)
    phi_w = got.transpose(2, 0, 1, 3).reshape(box, n * win, cells)
    own_planes = (ooff[None, :] + jnp.arange(box, dtype=jnp.int32)[:, None]) % planes
    pick = (own_planes[:, :, None] == jnp.arange(planes, dtype=jnp.int32)).astype(jnp.float32)
    local_pot = lax.dot_general(
        pick.reshape(-1, planes), potential.reshape(planes, cells),
        (((1,), (0,)), ((), ())), precision=highest,
    ).reshape(box, local, rows, depth)

    o = own.transpose(1, 0, 2, 3)
    ab = above.transpose(1, 0, 2, 3)
    be = below.transpose(1, 0, 2, 3)
    yy = jnp.concatenate([ab, o, be], axis=2)
    zz = jnp.pad(o, ((0, 0), (0, 0), (0, 0), (1, 1)))
    beside = yy[:, :, 2:] + yy[:, :, :-2] + zz[..., 2:] + zz[..., :-2]
    u = -0.5 * (beside - 6.0 * o) + local_pot * o - penalty * o
    xx = jnp.pad(o, ((1, 1), (0, 0), (0, 0), (0, 0)))
    base = (u - 0.5 * (xx[2:] + xx[:-2])).reshape(box, local, cells)
    o = o.reshape(box, local, cells)
    u = u.reshape(box, local, cells)

    pair = jnp.stack([u, o]).reshape(2 * box * local, cells)
    gram = lax.dot_general(
        pair, phi_w.reshape(box * n * win, cells), (((1,), (1,)), ((), ())),
        precision=highest,
    ).reshape(2, box, local, box, n * win)
    diff = (ooff[:, None] - woff[None, :]) % planes
    masks = {k: diff == k % planes for k in range(1 - box, box)}
    total = jnp.zeros((local, n * win), jnp.float32)
    for p in range(box):
        for q in range(box):
            total = total + jnp.where(masks[q - p], gram[0, p, :, q], 0.0)
            if q + 1 < box:
                total = total - jnp.where(masks[q + 1 - p], 0.5 * gram[1, p, :, q], 0.0)
            if q >= 1:
                total = total - jnp.where(masks[q - 1 - p], 0.5 * gram[1, p, :, q], 0.0)
    band = sub_sum(volume * total)
    mix = jnp.stack(
        [
            jnp.stack([jnp.where(masks[q - p], band, 0.0) for q in range(box)], axis=1)
            for p in range(box)
        ]
    )
    update = base.reshape(box * local, cells) - lax.dot_general(
        mix.reshape(box * local, box * n * win), phi_w.reshape(box * n * win, cells),
        (((1,), (0,)), ((), ())), precision=highest,
    )
    back = update.reshape(box, n, m, cells).transpose(1, 2, 0, 3)
    back = lax.all_to_all(back, "fn", 0, 0, tiled=True)
    return back.reshape(local, box, rows, depth)


def solution(mesh):
    return jax.shard_map(
        body,
        mesh=mesh,
        in_specs=(P("fn", None, "sub", None), P(), P(None, "sub", None)),
        out_specs=P("fn", None, "sub", None),
        check_vma=False,
    )
```

```python
import functools

import jax
import jax.numpy as jnp
from jax import lax
from jax.experimental import pallas as pl
from jax.experimental.pallas import tpu as pltpu
from jax.sharding import PartitionSpec as P

KMAX = 46
penalty = 0.5
VMEM = pl.BlockSpec(memory_space=pltpu.VMEM)


def split(x):
    hi = x.astype(jnp.bfloat16)
    return hi, (x - hi.astype(jnp.float32)).astype(jnp.bfloat16)


def dot_t(a, b):
    return lax.dot_general(a, b, (((1,), (1,)), ((), ())), preferred_element_type=jnp.float32)


def dot(a, b):
    return jnp.dot(a, b, preferred_element_type=jnp.float32)


def gram_kernel(
    box, rows, planes, volume,
    own_ref, left_ref, right_ref, above_ref, below_ref, pot_ref, ooff_ref, woff_ref,
    total_ref, base_ref, right_hand_ref,
    hi_ref, lo_ref,
):
    per = box * rows
    local = own_ref.shape[0] // per
    side = left_ref.shape[0] // per
    win = local + 2 * side
    depth = own_ref.shape[1]
    cells = rows * depth
    lane = lax.broadcasted_iota(jnp.int32, (local, depth), 1)
    plane_ids = lax.broadcasted_iota(jnp.int32, (local, planes), 1)
    ooff = ooff_ref[...]

    def piece(p, r):
        return own_ref[pl.ds(p * rows + r, local, stride=per), :]

    for p in range(box):
        wanted = ooff + p
        wanted = jnp.where(wanted >= planes, wanted - planes, wanted)
        pick = (plane_ids == wanted).astype(jnp.float32).astype(jnp.bfloat16)
        for r in range(rows):
            cols = pl.ds(r * depth, depth)
            o = piece(p, r)
            up = piece(p, r - 1) if r > 0 else above_ref[pl.ds(p, local, stride=box), :]
            down = piece(p, r + 1) if r < rows - 1 else below_ref[pl.ds(p, local, stride=box), :]
            zl = jnp.where(lane == 0, 0.0, pltpu.roll(o, 1, axis=1))
            zr = jnp.where(lane == depth - 1, 0.0, pltpu.roll(o, depth - 1, axis=1))
            pot_hi, pot_lo = split(pot_ref[pl.ds(r, planes, stride=rows), :])
            pot = dot(pick, pot_hi) + dot(pick, pot_lo)
            u = -0.5 * (up + down + zl + zr - 6.0 * o) + pot * o - penalty * o
            base = u
            if p > 0:
                base = base - 0.5 * piece(p - 1, r)
            if p < box - 1:
                base = base - 0.5 * piece(p + 1, r)
            base_ref[pl.ds(p * local, local), cols] = base
            u_hi, u_lo = split(u)
            hi_ref[pl.ds(p * local, local), cols] = u_hi
            lo_ref[pl.ds(p * local, local), cols] = u_lo
            o_hi, o_lo = split(o)
            hi_ref[pl.ds((box + p) * local, local), cols] = o_hi
            lo_ref[pl.ds((box + p) * local, local), cols] = o_lo
            low = pl.ds(cells + r * depth, depth)
            right_hand_ref[pl.ds(p * win + side, local), cols] = o_hi
            right_hand_ref[pl.ds(p * win + side, local), low] = o_lo
            for ref, at in ((left_ref, 0), (right_ref, side + local)):
                x_hi, x_lo = split(ref[pl.ds(p * rows + r, side, stride=per), :])
                right_hand_ref[pl.ds(p * win + at, side), cols] = x_hi
                right_hand_ref[pl.ds(p * win + at, side), low] = x_lo

    diff = ooff - woff_ref[...]
    masks = {}
    for k in range(1 - box, box):
        masks[k] = (diff == k) | (diff == k + planes) | (diff == k - planes)
    total = jnp.zeros((local, win), jnp.float32)
    for q in range(box):
        r_hi = right_hand_ref[pl.ds(q * win, win), pl.ds(0, cells)]
        r_lo = right_hand_ref[pl.ds(q * win, win), pl.ds(cells, cells)]
        for p in range(2 * box):
            at = pl.ds(p * local, local)
            l_hi, l_lo = hi_ref[at, :], lo_ref[at, :]
            gram = dot_t(l_hi, r_hi) + dot_t(l_hi, r_lo) + dot_t(l_lo, r_hi)
            if p < box:
                total = total + jnp.where(masks[q - p], gram, 0.0)
                continue
            if q + 1 < box:
                total = total - jnp.where(masks[q + 1 - p + box], 0.5 * gram, 0.0)
            if q >= 1:
                total = total - jnp.where(masks[q - 1 - p + box], 0.5 * gram, 0.0)
    total_ref[...] = volume * total


def mix_kernel(
    box, rows, planes,
    band_ref, base_ref, right_hand_ref, ooff_ref, woff_ref,
    out_ref,
    hi_ref, lo_ref,
):
    per = box * rows
    local, win = band_ref.shape
    cells = base_ref.shape[1]
    depth = cells // rows
    diff = ooff_ref[...] - woff_ref[...]
    b_hi, b_lo = split(band_ref[...])
    b_hi = b_hi.astype(jnp.float32)
    b_lo = b_lo.astype(jnp.float32)
    picked = {}
    for k in range(1 - box, box):
        mask = (diff == k) | (diff == k + planes) | (diff == k - planes)
        picked[k] = (
            jnp.where(mask, b_hi, 0.0).astype(jnp.bfloat16),
            jnp.where(mask, b_lo, 0.0).astype(jnp.bfloat16),
        )
    for p in range(box):
        update = base_ref[pl.ds(p * local, local), :]
        for q in range(box):
            r_hi = right_hand_ref[pl.ds(q * win, win), pl.ds(0, cells)]
            r_lo = right_hand_ref[pl.ds(q * win, win), pl.ds(cells, cells)]
            a_hi, a_lo = picked[q - p]
            update = update - (dot(a_hi, r_hi) + dot(a_hi, r_lo) + dot(a_lo, r_hi))
        for r in range(rows):
            out_ref[pl.ds(p * rows + r, local, stride=per), :] = update[:, r * depth : (r + 1) * depth]


def sub_edges(cells):
    count = lax.axis_size("sub")
    up = [(i, i + 1) for i in range(count - 1)]
    down = [(i + 1, i) for i in range(count - 1)]
    rows = cells.shape[2]
    above = lax.ppermute(cells[:, :, rows - 1], "sub", up)
    below = lax.ppermute(cells[:, :, 0], "sub", down)
    return above, below


def sub_sum(part):
    count = lax.axis_size("sub")
    step = 1
    while step < count:
        part = part + lax.ppermute(part, "sub", [(i, i ^ step) for i in range(count)])
        step *= 2
    return part


def body(coeffs, offsets, potential):
    n = lax.axis_size("fn")
    e = lax.axis_index("fn")
    local, box, rows, depth = coeffs.shape
    planes = potential.shape[0]
    cells = rows * depth
    m = local // n
    h = -(-(KMAX - 1) // n)
    side = h * n
    win = local + 2 * side
    volume = 1.0 / (box * 16 * 128)

    got = lax.all_to_all(coeffs.reshape(n, m, box, rows, depth), "fn", 0, 0, tiled=True)
    left = lax.ppermute(got[:, m - h :], "fn", [(i, (i + 1) % n) for i in range(n)])
    right = lax.ppermute(got[:, :h], "fn", [((i + 1) % n, i) for i in range(n)])
    above, below = sub_edges(got.reshape(local, box, rows, depth))

    offs = offsets.reshape(local, n)
    offs = jnp.concatenate([offs[local - h :], offs, offs[:h]], axis=0)
    woff = lax.dynamic_slice_in_dim(offs, m * e, m + 2 * h, axis=0)
    ooff = woff[h : h + m].T.reshape(local, 1)
    woff = jnp.concatenate(
        [woff[:h].T.reshape(1, side), ooff.reshape(1, local), woff[h + m :].T.reshape(1, side)],
        axis=1,
    )

    total, base, right_hand = pl.pallas_call(
        functools.partial(gram_kernel, box, rows, planes, volume),
        out_shape=(
            jax.ShapeDtypeStruct((local, win), jnp.float32),
            jax.ShapeDtypeStruct((box * local, cells), jnp.float32),
            jax.ShapeDtypeStruct((box * win, 2 * cells), jnp.bfloat16),
        ),
        in_specs=[VMEM] * 8,
        out_specs=(VMEM,) * 3,
        scratch_shapes=[pltpu.VMEM((2 * box * local, cells), jnp.bfloat16)] * 2,
        name="gram",
    )(
        got.reshape(-1, depth), left.reshape(-1, depth), right.reshape(-1, depth),
        above.reshape(-1, depth), below.reshape(-1, depth),
        potential.reshape(-1, depth), ooff, woff,
    )
    band = sub_sum(total)
    update = pl.pallas_call(
        functools.partial(mix_kernel, box, rows, planes),
        out_shape=jax.ShapeDtypeStruct((local * box * rows, depth), jnp.float32),
        in_specs=[VMEM] * 5,
        out_specs=VMEM,
        scratch_shapes=[pltpu.VMEM((8, 128), jnp.float32)] * 2,
        name="mix",
    )(band, base, right_hand, ooff, woff)
    back = lax.all_to_all(update.reshape(n, m, box, rows, depth), "fn", 0, 0, tiled=True)
    return back.reshape(local, box, rows, depth)


def solution(mesh):
    return jax.shard_map(
        body,
        mesh=mesh,
        in_specs=(P("fn", None, "sub", None), P(), P(None, "sub", None)),
        out_specs=P("fn", None, "sub", None),
        check_vma=False,
    )
```

```python
import functools

import jax
import jax.numpy as jnp
from jax import lax
from jax.experimental import pallas as pl
from jax.experimental.pallas import tpu as pltpu
from jax.sharding import PartitionSpec as P

KMAX = 46
penalty = 0.5
VMEM = pl.BlockSpec(memory_space=pltpu.VMEM)


def split(x):
    hi = x.astype(jnp.bfloat16)
    return hi, (x - hi.astype(jnp.float32)).astype(jnp.bfloat16)


def dot_t(a, b):
    return lax.dot_general(a, b, (((1,), (1,)), ((), ())), preferred_element_type=jnp.float32)


def dot(a, b):
    return jnp.dot(a, b, preferred_element_type=jnp.float32)


def dot3_t(l_hi, l_lo, r_hi, r_lo):
    return dot_t(l_hi, r_hi) + dot_t(l_hi, r_lo) + dot_t(l_lo, r_hi)


def delta_masks(box, planes, diff):
    return {
        k: (diff == k) | (diff == k + planes) | (diff == k - planes) for k in range(1 - box, box)
    }


def masked_sum(box, planes, diff, hi_ref, lo_ref, r_hi_ref, r_lo_ref, first):
    local, width = diff.shape
    masks = delta_masks(box, planes, diff)
    total = jnp.zeros((local, width), jnp.float32)
    for q0 in range(0, box, 2):
        at = pl.ds(first + q0 * width, 2 * width)
        grams = dot3_t(hi_ref[...], lo_ref[...], r_hi_ref[at, :], r_lo_ref[at, :])
        for q in (q0, q0 + 1):
            for p in range(box):
                cols = slice((q - q0) * width, (q - q0 + 1) * width)
                plain = grams[p * local : (p + 1) * local, cols]
                beside = 0.5 * grams[(box + p) * local : (box + p + 1) * local, cols]
                total = total + jnp.where(masks[q - p], plain, 0.0)
                if q + 1 < box:
                    total = total - jnp.where(masks[q + 1 - p], beside, 0.0) if q + 1 - p < box else total
                if q >= 1:
                    total = total - jnp.where(masks[q - 1 - p], beside, 0.0) if q - 1 - p > -box else total
    return total


def own_kernel(
    box, rows, planes,
    own_ref, above_ref, below_ref, pot_ref, ooff_ref, row_ref,
    total_ref, base_ref, hi_ref, lo_ref,
):
    per = box * rows
    local = own_ref.shape[0] // per
    depth = own_ref.shape[1]
    lane = lax.broadcasted_iota(jnp.int32, (local, depth), 1)
    plane_ids = lax.broadcasted_iota(jnp.int32, (local, planes), 1)
    ooff = ooff_ref[...]

    def piece(p, r):
        return own_ref[pl.ds(p * rows + r, local, stride=per), :]

    picks = []
    for p in range(box):
        wanted = ooff + p
        wanted = jnp.where(wanted >= planes, wanted - planes, wanted)
        picks.append((plane_ids == wanted).astype(jnp.float32).astype(jnp.bfloat16))
    picks = jnp.concatenate(picks, axis=0)
    for r in range(rows):
        cols = pl.ds(r * depth, depth)
        pot_hi, pot_lo = split(pot_ref[pl.ds(r, planes, stride=rows), :])
        pots = dot(picks, pot_hi) + dot(picks, pot_lo)
        for p in range(box):
            o = piece(p, r)
            up = piece(p, r - 1) if r > 0 else above_ref[pl.ds(p, local, stride=box), :]
            down = piece(p, r + 1) if r < rows - 1 else below_ref[pl.ds(p, local, stride=box), :]
            zl = jnp.where(lane == 0, 0.0, pltpu.roll(o, 1, axis=1))
            zr = jnp.where(lane == depth - 1, 0.0, pltpu.roll(o, depth - 1, axis=1))
            pot = pots[p * local : (p + 1) * local]
            u = -0.5 * (up + down + zl + zr - 6.0 * o) + pot * o - penalty * o
            base = u
            if p > 0:
                base = base - 0.5 * piece(p - 1, r)
            if p < box - 1:
                base = base - 0.5 * piece(p + 1, r)
            base_ref[pl.ds(p * local, local), cols] = base
            for value, at in ((u, p * local), (o, (box + p) * local)):
                x_hi, x_lo = split(value)
                hi_ref[pl.ds(at, local), cols] = x_hi
                lo_ref[pl.ds(at, local), cols] = x_lo
    diff = ooff - row_ref[...]
    total_ref[...] = masked_sum(box, planes, diff, hi_ref, lo_ref, hi_ref, lo_ref, box * local)


def side_kernel(
    box, rows, planes, volume,
    left_ref, right_ref, own_total_ref, hi_ref, lo_ref, ooff_ref, soff_ref,
    total_ref, s_hi_ref, s_lo_ref,
):
    per = box * rows
    side = left_ref.shape[0] // per
    depth = left_ref.shape[1]
    width = soff_ref.shape[1]
    local = ooff_ref.shape[0]
    for p in range(box):
        if width > 2 * side:
            pad = pl.ds(p * width + 2 * side, width - 2 * side)
            s_hi_ref[pad, :] = jnp.zeros((width - 2 * side, rows * depth), jnp.bfloat16)
            s_lo_ref[pad, :] = jnp.zeros((width - 2 * side, rows * depth), jnp.bfloat16)
        for r in range(rows):
            cols = pl.ds(r * depth, depth)
            for ref, at in ((left_ref, 0), (right_ref, side)):
                x_hi, x_lo = split(ref[pl.ds(p * rows + r, side, stride=per), :])
                s_hi_ref[pl.ds(p * width + at, side), cols] = x_hi
                s_lo_ref[pl.ds(p * width + at, side), cols] = x_lo
    diff = ooff_ref[...] - soff_ref[...]
    total = masked_sum(box, planes, diff, hi_ref, lo_ref, s_hi_ref, s_lo_ref, 0)
    total_ref[:, pl.ds(0, local)] = volume * own_total_ref[...]
    total_ref[:, pl.ds(local, width)] = volume * total


def mix_kernel(
    box, rows, planes,
    band_ref, base_ref, hi_ref, lo_ref, s_hi_ref, s_lo_ref, ooff_ref, row_ref, soff_ref,
    out_ref,
    own_hi, own_lo, side_hi, side_lo,
):
    per = box * rows
    local = ooff_ref.shape[0]
    width = soff_ref.shape[1]
    depth = out_ref.shape[1]
    ooff = ooff_ref[...]
    for diff, start, to_hi, to_lo in (
        (ooff - row_ref[...], 0, own_hi, own_lo),
        (ooff - soff_ref[...], local, side_hi, side_lo),
    ):
        size = diff.shape[1]
        masks = delta_masks(box, planes, diff)
        band = band_ref[:, pl.ds(start, size)]
        for k in range(1 - box, box):
            x_hi, x_lo = split(jnp.where(masks[k], band, 0.0))
            for p in range(box):
                q = p + k
                if 0 <= q < box:
                    to_hi[pl.ds(p * local, local), pl.ds(q * size, size)] = x_hi
                    to_lo[pl.ds(p * local, local), pl.ds(q * size, size)] = x_lo
    own = pl.ds(box * local, box * local)
    r_hi, r_lo = hi_ref[own, :], lo_ref[own, :]
    update = base_ref[...] - (
        dot(own_hi[...], r_hi) + dot(own_hi[...], r_lo) + dot(own_lo[...], r_hi)
        + dot(side_hi[...], s_hi_ref[...]) + dot(side_hi[...], s_lo_ref[...])
        + dot(side_lo[...], s_hi_ref[...])
    )
    for p in range(box):
        for r in range(rows):
            out_ref[pl.ds(p * rows + r, local, stride=per), :] = update[
                p * local : (p + 1) * local, r * depth : (r + 1) * depth
            ]


def sub_edges(cells):
    count = lax.axis_size("sub")
    up = [(i, i + 1) for i in range(count - 1)]
    down = [(i + 1, i) for i in range(count - 1)]
    rows = cells.shape[2]
    above = lax.ppermute(cells[:, :, rows - 1], "sub", up)
    below = lax.ppermute(cells[:, :, 0], "sub", down)
    return above, below


def sub_sum(part):
    count = lax.axis_size("sub")
    step = 1
    while step < count:
        part = part + lax.ppermute(part, "sub", [(i, i ^ step) for i in range(count)])
        step *= 2
    return part


def body(coeffs, offsets, potential):
    n = lax.axis_size("fn")
    e = lax.axis_index("fn")
    local, box, rows, depth = coeffs.shape
    planes = potential.shape[0]
    cells = rows * depth
    m = local // n
    h = -(-(KMAX - 1) // n)
    side = h * n
    volume = 1.0 / (box * 16 * 128)

    got = lax.all_to_all(coeffs.reshape(n, m, box, rows, depth), "fn", 0, 0, tiled=True)
    left = lax.ppermute(got[:, m - h :], "fn", [(i, (i + 1) % n) for i in range(n)])
    right = lax.ppermute(got[:, :h], "fn", [((i + 1) % n, i) for i in range(n)])
    above, below = sub_edges(got.reshape(local, box, rows, depth))

    offs = offsets.reshape(local, n)
    offs = jnp.concatenate([offs[local - h :], offs, offs[:h]], axis=0)
    woff = lax.dynamic_slice_in_dim(offs, m * e, m + 2 * h, axis=0)
    ooff = woff[h : h + m].T.reshape(local, 1)
    row = ooff.reshape(1, local)
    width = -(-2 * side // 128) * 128
    soff = jnp.concatenate(
        [
            woff[:h].T.reshape(1, side),
            woff[h + m :].T.reshape(1, side),
            jnp.full((1, width - 2 * side), -8 * planes, jnp.int32),
        ],
        axis=1,
    )
    params = pltpu.CompilerParams(vmem_limit_bytes=28 * 2**20)
    f32, bf16 = jnp.float32, jnp.bfloat16
    shape = jax.ShapeDtypeStruct
    full = (2 * box * local, cells)
    own_total, base, hi, lo = pl.pallas_call(
        functools.partial(own_kernel, box, rows, planes),
        out_shape=(
            shape((local, local), f32), shape((box * local, cells), f32),
            shape(full, bf16), shape(full, bf16),
        ),
        in_specs=[VMEM] * 6,
        out_specs=(VMEM,) * 4,
        compiler_params=params,
        cost_estimate=pl.CostEstimate(
            flops=12 * box * box * local * local * cells, bytes_accessed=8 * 2**20, transcendentals=0
        ),
        name="own",
    )(
        got.reshape(-1, depth), above.reshape(-1, depth), below.reshape(-1, depth),
        potential.reshape(-1, depth), ooff, row,
    )
    total, s_hi, s_lo = pl.pallas_call(
        functools.partial(side_kernel, box, rows, planes, volume),
        out_shape=(
            shape((local, local + width), f32),
            shape((box * width, cells), bf16), shape((box * width, cells), bf16),
        ),
        in_specs=[VMEM] * 7,
        out_specs=(VMEM,) * 3,
        compiler_params=params,
        name="side",
    )(left.reshape(-1, depth), right.reshape(-1, depth), own_total, hi, lo, ooff, soff)
    band = sub_sum(total)
    update = pl.pallas_call(
        functools.partial(mix_kernel, box, rows, planes),
        out_shape=shape((local * box * rows, depth), f32),
        in_specs=[VMEM] * 9,
        out_specs=VMEM,
        scratch_shapes=[pltpu.VMEM((box * local, box * local), bf16)] * 2
        + [pltpu.VMEM((box * local, box * width), bf16)] * 2,
        compiler_params=params,
        name="mix",
    )(band, base, hi, lo, s_hi, s_lo, ooff, row, soff)
    back = lax.all_to_all(update.reshape(n, m, box, rows, depth), "fn", 0, 0, tiled=True)
    return back.reshape(local, box, rows, depth)


def solution(mesh):
    return jax.shard_map(
        body,
        mesh=mesh,
        in_specs=(P("fn", None, "sub", None), P(), P(None, "sub", None)),
        out_specs=P("fn", None, "sub", None),
        check_vma=False,
    )
```

```python
import functools

import jax
import jax.numpy as jnp
from jax import lax
from jax.experimental import pallas as pl
from jax.experimental.pallas import tpu as pltpu
from jax.sharding import PartitionSpec as P


KMAX = 46
penalty = 0.5
VMEM = pl.BlockSpec(memory_space=pltpu.VMEM)


def split(x):
    hi = x.astype(jnp.bfloat16)
    return hi, (x - hi.astype(jnp.float32)).astype(jnp.bfloat16)


def dot_t(a, b):
    return lax.dot_general(a, b, (((1,), (1,)), ((), ())), preferred_element_type=jnp.float32)


def dot(a, b):
    return jnp.dot(a, b, preferred_element_type=jnp.float32)


def dot3_t(l_hi, l_lo, r_hi, r_lo):
    return dot_t(l_hi, r_hi) + dot_t(l_hi, r_lo) + dot_t(l_lo, r_hi)


def delta_masks(box, planes, diff):
    return {
        k: (diff == k) | (diff == k + planes) | (diff == k - planes) for k in range(1 - box, box)
    }


def masked_sum(box, planes, diff, hi_ref, lo_ref, r_hi_ref, r_lo_ref, first):
    local, width = diff.shape
    masks = delta_masks(box, planes, diff)
    total = jnp.zeros((local, width), jnp.float32)
    for q0 in range(0, box, 2):
        at = pl.ds(first + q0 * width, 2 * width)
        grams = dot3_t(hi_ref[...], lo_ref[...], r_hi_ref[at, :], r_lo_ref[at, :])
        for q in (q0, q0 + 1):
            for p in range(box):
                cols = slice((q - q0) * width, (q - q0 + 1) * width)
                plain = grams[p * local : (p + 1) * local, cols]
                beside = 0.5 * grams[(box + p) * local : (box + p + 1) * local, cols]
                total = total + jnp.where(masks[q - p], plain, 0.0)
                if q + 1 < box:
                    total = total - jnp.where(masks[q + 1 - p], beside, 0.0) if q + 1 - p < box else total
                if q >= 1:
                    total = total - jnp.where(masks[q - 1 - p], beside, 0.0) if q - 1 - p > -box else total
    return total


def own_kernel(
    box, rows, planes,
    own_ref, above_ref, below_ref, pot_ref, ooff_ref, row_ref,
    total_ref, base_ref, hi_ref, lo_ref,
):
    per = box * rows
    local = own_ref.shape[0] // per
    depth = own_ref.shape[1]
    lane = lax.broadcasted_iota(jnp.int32, (local, depth), 1)
    plane_ids = lax.broadcasted_iota(jnp.int32, (local, planes), 1)
    ooff = ooff_ref[...]

    def piece(p, r):
        return own_ref[pl.ds(p * rows + r, local, stride=per), :]

    picks = []
    for p in range(box):
        wanted = ooff + p
        wanted = jnp.where(wanted >= planes, wanted - planes, wanted)
        picks.append((plane_ids == wanted).astype(jnp.float32).astype(jnp.bfloat16))
    picks = jnp.concatenate(picks, axis=0)
    for r in range(rows):
        cols = pl.ds(r * depth, depth)
        pot_hi, pot_lo = split(pot_ref[pl.ds(r, planes, stride=rows), :])
        pots = dot(picks, pot_hi) + dot(picks, pot_lo)
        for p in range(box):
            o = piece(p, r)
            up = piece(p, r - 1) if r > 0 else above_ref[pl.ds(p, local, stride=box), :]
            down = piece(p, r + 1) if r < rows - 1 else below_ref[pl.ds(p, local, stride=box), :]
            zl = jnp.where(lane == 0, 0.0, pltpu.roll(o, 1, axis=1))
            zr = jnp.where(lane == depth - 1, 0.0, pltpu.roll(o, depth - 1, axis=1))
            pot = pots[p * local : (p + 1) * local]
            u = -0.5 * (up + down + zl + zr - 6.0 * o) + pot * o - penalty * o
            base = u
            if p > 0:
                base = base - 0.5 * piece(p - 1, r)
            if p < box - 1:
                base = base - 0.5 * piece(p + 1, r)
            base_ref[pl.ds(p * local, local), cols] = base
            for value, at in ((u, p * local), (o, (box + p) * local)):
                x_hi, x_lo = split(value)
                hi_ref[pl.ds(at, local), cols] = x_hi
                lo_ref[pl.ds(at, local), cols] = x_lo
    diff = ooff - row_ref[...]
    total_ref[...] = masked_sum(box, planes, diff, hi_ref, lo_ref, hi_ref, lo_ref, box * local)


def side_kernel(
    box, rows, planes, volume,
    left_ref, right_ref, own_total_ref, hi_ref, lo_ref, ooff_ref, soff_ref,
    total_ref, s_hi_ref, s_lo_ref,
):
    per = box * rows
    side = left_ref.shape[0] // per
    depth = left_ref.shape[1]
    width = soff_ref.shape[1]
    local = ooff_ref.shape[0]
    for p in range(box):
        if width > 2 * side:
            pad = pl.ds(p * width + 2 * side, width - 2 * side)
            s_hi_ref[pad, :] = jnp.zeros((width - 2 * side, rows * depth), jnp.bfloat16)
            s_lo_ref[pad, :] = jnp.zeros((width - 2 * side, rows * depth), jnp.bfloat16)
        for r in range(rows):
            cols = pl.ds(r * depth, depth)
            for ref, at in ((left_ref, 0), (right_ref, side)):
                x_hi, x_lo = split(ref[pl.ds(p * rows + r, side, stride=per), :])
                s_hi_ref[pl.ds(p * width + at, side), cols] = x_hi
                s_lo_ref[pl.ds(p * width + at, side), cols] = x_lo
    diff = ooff_ref[...] - soff_ref[...]
    total = masked_sum(box, planes, diff, hi_ref, lo_ref, s_hi_ref, s_lo_ref, 0)
    total_ref[:, pl.ds(0, local)] = volume * own_total_ref[...]
    total_ref[:, pl.ds(local, width)] = volume * total


def mix_kernel(
    box, rows, planes,
    band_ref, base_ref, hi_ref, lo_ref, s_hi_ref, s_lo_ref, ooff_ref, row_ref, soff_ref,
    out_ref,
    own_hi, own_lo, side_hi, side_lo,
):
    per = box * rows
    local = ooff_ref.shape[0]
    depth = out_ref.shape[1]
    ooff = ooff_ref[...]
    for diff, start, to_hi, to_lo in (
        (ooff - row_ref[...], 0, own_hi, own_lo),
        (ooff - soff_ref[...], local, side_hi, side_lo),
    ):
        size = diff.shape[1]
        masks = delta_masks(box, planes, diff)
        band = band_ref[:, pl.ds(start, size)]
        for k in range(1 - box, box):
            x_hi, x_lo = split(jnp.where(masks[k], band, 0.0))
            for p in range(box):
                q = p + k
                if 0 <= q < box:
                    to_hi[pl.ds(p * local, local), pl.ds(q * size, size)] = x_hi
                    to_lo[pl.ds(p * local, local), pl.ds(q * size, size)] = x_lo
    own = pl.ds(box * local, box * local)
    r_hi, r_lo = hi_ref[own, :], lo_ref[own, :]
    update = base_ref[...] - (
        dot(own_hi[...], r_hi) + dot(own_hi[...], r_lo) + dot(own_lo[...], r_hi)
        + dot(side_hi[...], s_hi_ref[...]) + dot(side_hi[...], s_lo_ref[...])
        + dot(side_lo[...], s_hi_ref[...])
    )
    for p in range(box):
        for r in range(rows):
            out_ref[pl.ds(p * rows + r, local, stride=per), :] = update[
                p * local : (p + 1) * local, r * depth : (r + 1) * depth
            ]


def sub_edges(cells):
    count = lax.axis_size("sub")
    up = [(i, i + 1) for i in range(count - 1)]
    down = [(i + 1, i) for i in range(count - 1)]
    rows = cells.shape[2]
    above = lax.ppermute(cells[:, :, rows - 1], "sub", up)
    below = lax.ppermute(cells[:, :, 0], "sub", down)
    return above, below


def sub_sum(part):
    count = lax.axis_size("sub")
    step = 1
    while step < count:
        part = part + lax.ppermute(part, "sub", [(i, i ^ step) for i in range(count)])
        step *= 2
    return part


def body(coeffs, offsets, potential):
    n = lax.axis_size("fn")
    e = lax.axis_index("fn")
    local, box, rows, depth = coeffs.shape
    planes = potential.shape[0]
    cells = rows * depth
    m = local // n
    h = -(-(KMAX - 1) // n)
    side = h * n
    volume = 1.0 / (box * 16 * 128)

    got = lax.all_to_all(coeffs.reshape(n, m, box, rows, depth), "fn", 0, 0, tiled=True)
    tail, head, after = lax.optimization_barrier((got[:, m - h :], got[:, :h], got))
    left = lax.ppermute(tail, "fn", [(i, (i + 1) % n) for i in range(n)])
    right = lax.ppermute(head, "fn", [((i + 1) % n, i) for i in range(n)])
    above, below = sub_edges(after.reshape(local, box, rows, depth))

    offs = offsets.reshape(local, n)
    offs = jnp.concatenate([offs[local - h :], offs, offs[:h]], axis=0)
    woff = lax.dynamic_slice_in_dim(offs, m * e, m + 2 * h, axis=0)
    ooff = woff[h : h + m].T.reshape(local, 1)
    row = ooff.reshape(1, local)
    width = -(-2 * side // 128) * 128
    soff = jnp.concatenate(
        [
            woff[:h].T.reshape(1, side),
            woff[h + m :].T.reshape(1, side),
            jnp.full((1, width - 2 * side), -8 * planes, jnp.int32),
        ],
        axis=1,
    )
    params = pltpu.CompilerParams(vmem_limit_bytes=28 * 2**20)
    f32, bf16 = jnp.float32, jnp.bfloat16
    shape = jax.ShapeDtypeStruct
    full = (2 * box * local, cells)
    own_total, base, hi, lo = pl.pallas_call(
        functools.partial(own_kernel, box, rows, planes),
        out_shape=(
            shape((local, local), f32), shape((box * local, cells), f32),
            shape(full, bf16), shape(full, bf16),
        ),
        in_specs=[VMEM] * 6,
        out_specs=(VMEM,) * 4,
        compiler_params=params,
        cost_estimate=pl.CostEstimate(
            flops=12 * box * box * local * local * cells, bytes_accessed=8 * 2**20, transcendentals=0
        ),
        name="own",
    )(
        got.reshape(-1, depth), above.reshape(-1, depth), below.reshape(-1, depth),
        potential.reshape(-1, depth), ooff, row,
    )
    total, s_hi, s_lo = pl.pallas_call(
        functools.partial(side_kernel, box, rows, planes, volume),
        out_shape=(
            shape((local, local + width), f32),
            shape((box * width, cells), bf16), shape((box * width, cells), bf16),
        ),
        in_specs=[VMEM] * 7,
        out_specs=(VMEM,) * 3,
        compiler_params=params,
        name="side",
    )(left.reshape(-1, depth), right.reshape(-1, depth), own_total, hi, lo, ooff, soff)
    band = sub_sum(total)
    update = pl.pallas_call(
        functools.partial(mix_kernel, box, rows, planes),
        out_shape=shape((local * box * rows, depth), f32),
        in_specs=[VMEM] * 9,
        out_specs=VMEM,
        scratch_shapes=[pltpu.VMEM((box * local, box * local), bf16)] * 2
        + [pltpu.VMEM((box * local, box * width), bf16)] * 2,
        compiler_params=params,
        name="mix",
    )(band, base, hi, lo, s_hi, s_lo, ooff, row, soff)
    back = lax.all_to_all(update.reshape(n, m, box, rows, depth), "fn", 0, 0, tiled=True)
    return back.reshape(local, box, rows, depth)


def solution(mesh):
    return jax.shard_map(
        body,
        mesh=mesh,
        in_specs=(P("fn", None, "sub", None), P(), P(None, "sub", None)),
        out_specs=P("fn", None, "sub", None),
        check_vma=False,
    )
```
